256 devices in a mesh: rows: 64 (over y, x_hi, z), tgt: 4 (over x_lo, core).
Axes of the slice: x: 4 (x_hi: 2, x_lo: 2; x = x_hi * 2 + x_lo), y: 4, z: 8, core: 2. Of those that a mesh axis runs over, the one named last changes fastest.
Arguments:
- frames: bfloat16 [512, 256, 128], P('rows', 'tgt'), may hold values from -8 to 8
- window: int32 [64, 3], P('rows'), may hold values from 0 to 1, as said below
- patch_embed_weight: bfloat16 [64, 128], replicated, may hold values from -0.75 to 0.75
- dilated_conv_weight: bfloat16 [9, 128, 128], replicated, may hold values from -0.1875 to 0.1875
- context_gate_weight: bfloat16 [128, 384], replicated, may hold values from -0.1875 to 0.1875
- hidden_gate_weight: bfloat16 [9, 128, 256], replicated, may hold values from -0.25 to 0.25
- candidate_weight: bfloat16 [128, 128], replicated, may hold values from -1 to 1
- motion_gate_weight: float32 [2, 384], replicated, may hold values from -0.75 to 0.75
- motion_head_weight: float32 [128, 2], replicated, may hold values from -0.5 to 0.5
Outputs:
- motion: float32 [2, 512, 256], P(None, 'rows', 'tgt')
- hidden: bfloat16 [512, 256, 128], P('rows', 'tgt')
The draws below stay inside these ranges and needn't reach their ends.
Inputs may be any that keep to these rules, and one draw needn't show every extreme that they name: `window`: entry o of a band's row says whether target band (band + o - 1) is searched; the middle entry is always 1.
All inputs are finite; a program needn't handle non-finite values.
Results may differ from the reference program's by a relative error of at most 0.015.
The reference program's roundings to bfloat16 on the way count: a program that leaves them out, or rounds other values in their place, can miss the bound.
Values may be sent and summed in bfloat16 or wider, within the bound.
A program may use at most 64 MiB of HBM per device.

```python
import math
import jax
import jax.numpy as jnp
from jax import lax

FEATURE_CHANNELS = 128
HID = 128
PATCH = 64
KERNEL_TAPS = 9
NOFF = 3
ITERS = 3
BH = 8
NB = 64
HT = 512
WT = 256


def draw_frames(key, part):
    first_key, noise_key, shift_key = jax.random.split(key, 3)
    shift_by = jax.random.randint(shift_key, (2,), -2, 3)
    first_frame = jax.random.normal(first_key, (HT, WT, PATCH), jnp.float32)
    noise_part = 0.6 * jax.random.normal(noise_key, (HT, WT, PATCH), jnp.float32)
    second_frame = 0.8 * jnp.roll(first_frame, (shift_by[0], shift_by[1]), axis=(0, 1)) + noise_part
    joined = jnp.concatenate([first_frame, second_frame], axis=2)
    return jnp.clip(joined, -8.0, 8.0).astype(jnp.bfloat16)


def draw_window(key, part):
    drawn = jnp.minimum(jax.random.randint(key, (NB, NOFF), 0, 4), 1)
    middle = (jnp.arange(NOFF, dtype=jnp.int32) == NOFF // 2)[None, :]
    return jnp.where(middle, 1, drawn).astype(jnp.int32)


def draw_hidden_gate_weight(key, part):
    own_key = jax.random.fold_in(key, 7)
    shape = (KERNEL_TAPS, HID, 2 * HID)
    drawn = jnp.clip(0.12 * jax.random.normal(own_key, shape, jnp.float32), -0.25, 0.25)
    return drawn.astype(jnp.bfloat16)


def scatter_about(rng, dims, width, limit, held_as=jnp.bfloat16):
    return jnp.clip(width * jax.random.normal(rng, dims, jnp.float32), -limit, limit).astype(held_as)


def setup_inputs(seed: int = 0) -> dict:
    splits = jax.random.split(jax.random.key(seed), 10)
    return {
        "frames": draw_frames(jax.random.fold_in(splits[9], 71), 0),
        "window": draw_window(jax.random.fold_in(splits[9], 71), 0),
        "patch_embed_weight": scatter_about(splits[2], (PATCH, FEATURE_CHANNELS), PATCH ** -0.5, 0.75),
        "dilated_conv_weight": scatter_about(splits[3], (KERNEL_TAPS, FEATURE_CHANNELS, FEATURE_CHANNELS), (KERNEL_TAPS * FEATURE_CHANNELS) ** -0.5, 0.1875),
        "context_gate_weight": scatter_about(splits[4], (FEATURE_CHANNELS, 3 * HID), (9 * FEATURE_CHANNELS) ** -0.5, 0.1875),
        "hidden_gate_weight": draw_hidden_gate_weight(jax.random.fold_in(splits[9], 71), 0),
        "candidate_weight": scatter_about(splits[6], (HID, HID), (HID // 4) ** -0.5, 1.0),
        "motion_gate_weight": scatter_about(splits[7], (2, 3 * HID), 0.3, 0.75, jnp.float32),
        "motion_head_weight": scatter_about(splits[8], (HID, 2), HID ** -0.5, 0.5, jnp.float32),
    }


def kernel_tap_sum(padded_features, weights, grid_height, grid_width, stride):
    summed_taps = None
    for row_tap in range(3):
        for col_tap in range(3):
            tap_piece = padded_features[..., stride * row_tap:stride * row_tap + grid_height, stride * col_tap:stride * col_tap + grid_width, :]
            tap_term = jnp.dot(tap_piece, weights[3 * row_tap + col_tap], preferred_element_type=jnp.float32)
            summed_taps = tap_term if summed_taps is None else summed_taps + tap_term
    return summed_taps

def encode_frame_pair(frames, patch_embed_weight, dilated_conv_weight):
    half_width = frames.shape[-1] // 2
    first_frame = jnp.dot(frames[..., :half_width], patch_embed_weight, preferred_element_type=jnp.float32)
    second_frame = jnp.dot(frames[..., half_width:], patch_embed_weight, preferred_element_type=jnp.float32)
    encoded_frames = jnp.stack([first_frame, second_frame]).astype(jnp.bfloat16)
    grid_height, grid_width = (encoded_frames.shape[1], encoded_frames.shape[2])
    padded_features = jnp.pad(encoded_frames, ((0, 0), (2, 2), (2, 2), (0, 0)))
    summed_taps = kernel_tap_sum(padded_features, dilated_conv_weight, grid_height, grid_width, 2)
    return (encoded_frames.astype(jnp.float32) + jax.nn.relu(summed_taps)).astype(jnp.bfloat16)

def tile_flow(band_index, source_all, padded_targets, window):
    grid_width = source_all.shape[1]
    channels = source_all.shape[2]
    source = lax.dynamic_slice_in_dim(source_all, band_index * BH, BH, 0).reshape(BH * grid_width, channels).astype(jnp.float32)
    targets = lax.dynamic_slice_in_dim(padded_targets, band_index * BH, 3 * BH, 0).reshape(3, BH * grid_width, channels).astype(jnp.float32)
    scores = jnp.einsum('ic,ojc->oij', source, targets) * (1.0 / math.sqrt(channels))
    offsets = jnp.arange(3, dtype=jnp.int32) - 1
    neighbour = band_index + offsets
    window_row = lax.dynamic_index_in_dim(window, band_index, 0, keepdims=False)
    allowed = (window_row == 1) & (neighbour >= 0) & (neighbour < NB)
    masked = jnp.where(allowed[:, None, None], scores, -jnp.inf)
    largest = lax.optimization_barrier(jnp.max(masked, axis=(0, 2)))
    row_pot = -(largest + jnp.log(lax.optimization_barrier(jnp.sum(jnp.exp(masked - largest[None, :, None]), axis=(0, 2)))))
    shifted = scores + row_pot[None, :, None]
    col_top = lax.optimization_barrier(jnp.max(shifted, axis=1))
    col_pot = -(col_top + jnp.log(lax.optimization_barrier(jnp.sum(jnp.exp(shifted - col_top[:, None, :]), axis=1))))
    coupling = jnp.where(allowed[:, None, None], jnp.exp(shifted + col_pot[:, None, :]), 0.0)
    weight_sum = lax.optimization_barrier(jnp.sum(coupling, axis=(0, 2)))
    cell_ids = jnp.arange(BH * grid_width, dtype=jnp.int32)
    cell_row = (cell_ids // grid_width).astype(jnp.float32)
    cell_col = (cell_ids % grid_width).astype(jnp.float32)
    row_shift = (offsets.astype(jnp.float32) * BH)[:, None, None] + cell_row[None, None, :] - cell_row[None, :, None]
    col_shift = cell_col[None, None, :] - cell_col[None, :, None]
    flow_row = lax.optimization_barrier(jnp.sum(coupling * row_shift, axis=(0, 2))) / weight_sum
    flow_col = lax.optimization_barrier(jnp.sum(coupling * col_shift, axis=(0, 2))) / weight_sum
    return jnp.stack([flow_row, flow_col]).reshape(2, BH, grid_width)

def reference(frames, window, patch_embed_weight, dilated_conv_weight, context_gate_weight, hidden_gate_weight, candidate_weight, motion_gate_weight, motion_head_weight):
    feature_maps = encode_frame_pair(frames, patch_embed_weight, dilated_conv_weight)
    grid_height, grid_width = (feature_maps.shape[1], feature_maps.shape[2])
    padded_targets = jnp.pad(feature_maps[1], ((BH, BH), (0, 0), (0, 0)))

    def one_tile(band_index):
        return tile_flow(band_index, feature_maps[0], padded_targets, window)
    tile_flows = lax.map(one_tile, jnp.arange(NB, dtype=jnp.int32))
    motion = jnp.transpose(tile_flows, (1, 0, 2, 3)).reshape(2, grid_height, grid_width)
    hidden_w = candidate_weight.shape[0]
    context = feature_maps[0]
    hidden = jnp.tanh(context.astype(jnp.float32)).astype(jnp.bfloat16)
    context_drive = jnp.dot(context, context_gate_weight, preferred_element_type=jnp.float32)
    for iteration in range(ITERS):
        padded_features = jnp.pad(hidden, ((1, 1), (1, 1), (0, 0)))
        from_flow = motion[0][..., None] * motion_gate_weight[0] + motion[1][..., None] * motion_gate_weight[1]
        gate_values = jax.nn.sigmoid(kernel_tap_sum(padded_features, hidden_gate_weight, grid_height, grid_width, 1) + context_drive[..., :2 * hidden_w] + from_flow[..., :2 * hidden_w])
        update = gate_values[..., :hidden_w]
        reset_gate = gate_values[..., hidden_w:]
        reset_hidden = (reset_gate * hidden.astype(jnp.float32)).astype(jnp.bfloat16)
        candidate = jnp.tanh(jnp.dot(reset_hidden, candidate_weight, preferred_element_type=jnp.float32) + context_drive[..., 2 * hidden_w:] + from_flow[..., 2 * hidden_w:])
        hidden = ((1.0 - update) * hidden.astype(jnp.float32) + update * candidate).astype(jnp.bfloat16)
        increment = jnp.dot(hidden.astype(jnp.float32), motion_head_weight, precision=lax.Precision.HIGHEST)
        motion = motion + jnp.moveaxis(increment, -1, 0)
    return (motion, hidden)
```

```python
import functools
import math

import jax
import jax.numpy as jnp
from jax import lax
from jax.experimental import pallas as pl
from jax.experimental.pallas import tpu as pltpu
from jax.sharding import PartitionSpec as P

BF = jnp.bfloat16
F32 = jnp.float32
LOG2E = 1.4426950408889634
BAND = 8
COLS = 64
WIDE = 256
CH = 128
PADW = 96
MINUS, PLUS = -1, 1


def roll0(x, shift):
    return pltpu.roll(x, shift % x.shape[0], axis=0)


def dot(a, b):
    return jnp.dot(a, b, preferred_element_type=F32)


def dot_nt(a, b):
    return lax.dot_general(a, b, (((1,), (1,)), ((), ())), preferred_element_type=F32)


def placement(rows, halo, side):
    token = lax.broadcasted_iota(jnp.int32, (rows * 16, 48), 0)
    strip = lax.broadcasted_iota(jnp.int32, (rows * 16, 48), 1)
    row, col = token >> 4, token & 15
    base = 2 * (row + 8 - halo)
    if side == 0:
        hit = (col >= 14) & (strip == base + col - 14)
    else:
        hit = (col < 2) & (strip == base + col)
    return jnp.where(hit, 1.0, 0.0).astype(BF)


def strip_pick():
    strip = lax.broadcasted_iota(jnp.int32, (32, BAND * COLS), 0)
    token = lax.broadcasted_iota(jnp.int32, (32, BAND * COLS), 1)
    row, col = (strip & 15) >> 1, strip & 1
    wanted = row * COLS + col + jnp.where(strip >= 16, COLS - 2, 0)
    return jnp.where(token == wanted, 1.0, 0.0).astype(BF)


def kernel(
    n_rows,
    frames,
    window,
    patch_w,
    dil_w,
    ctx_w,
    gate_w,
    cand_w,
    mgate_w,
    mhead_w,
    motion_out,
    hidden_out,
    raw,
    e1,
    f1,
    sb,
    qb,
    rp,
    e0,
    hp,
    sbuf,
    sx,
    st,
    sr,
    gs,
    rowmax,
    rowsum,
    f0,
    drive,
    wc,
    wh,
    hw,
    acc,
    raw_send,
    raw_recv,
    fwd_send,
    fwd_recv,
    halo_send,
    halo_recv,
    col_send,
    col_recv,
):
    r = lax.axis_index("rows")
    t = lax.axis_index("tgt")
    sib = t + 1 - 2 * (t % 2)
    far = (t + 2) % 4
    far_sib = 3 - t

    def row_ok(d):
        return (r + d >= 0) & (r + d < n_rows)

    def col_ok(d):
        return (t + d >= 0) & (t + d < 4)

    def remote(src, dst, send, recv, rr, tt):
        return pltpu.make_async_remote_copy(
            src_ref=src,
            dst_ref=dst,
            send_sem=send,
            recv_sem=recv,
            device_id=(rr, tt),
            device_id_type=pl.DeviceIdType.MESH,
        )

    def zero(ref):
        ref[...] = jnp.zeros(ref.shape, ref.dtype)

    for b in (t, far):
        for d, lo, hi in ((-1, 2, 10), (-2, 0, 2), (1, 18, 26), (2, 26, 28)):

            @pl.when(jnp.logical_not(row_ok(d)))
            def _():
                zero(raw.at[b, lo:hi])

    for d, rp_lo, rp_hi, hp_row, slot in ((-1, 0, 2, 0, 0), (1, 10, 12, 9, 2)):

        @pl.when(jnp.logical_not(row_ok(d)))
        def _():
            rp[rp_lo:rp_hi, 16:80] = jnp.zeros((2, COLS, CH), BF)
            for e in range(3):
                hp[e, hp_row, 16:80] = jnp.zeros((COLS, CH), BF)
            for e in range(4):
                for side in range(2):
                    zero(sx.at[e, side, slot])

    for d, side in ((-1, 0), (1, 1)):

        @pl.when(jnp.logical_not(col_ok(d)))
        def _():
            for e in range(4):
                for slot in range(3):
                    zero(sx.at[e, side, slot])

    barrier = pltpu.get_barrier_semaphore()
    count = 3

    def greet(rr, tt):
        pl.semaphore_signal(
            barrier, inc=1, device_id=(rr, tt), device_id_type=pl.DeviceIdType.MESH
        )

    for tt in (far, sib, far_sib):
        greet(r, tt)
    for d in (1, -1, 2, -2):
        partners = (t, far) if abs(d) == 2 else (t, far, sib, far_sib)

        @pl.when(row_ok(d))
        def _():
            for tt in partners:
                greet(r + d, tt)

        count = count + len(partners) * row_ok(d).astype(jnp.int32)

    whole = frames[...].astype(F32)
    half0 = whole[:, 0:32].reshape(BAND * 32, CH)
    half1 = whole[:, 32:64].reshape(BAND * 32, CH)
    lane = lax.broadcasted_iota(jnp.int32, (BAND * 32, CH), 1)
    packed = jnp.where(lane < 64, pltpu.roll(half0, 64, axis=1), half1)
    raw[t, 10:18] = packed.astype(BF).reshape(BAND, 32, CH)
    pick = strip_pick()
    sbuf[0] = dot(pick, frames[...].reshape(BAND * COLS, CH)).astype(BF).reshape(2, 16, CH)

    pl.semaphore_wait(barrier, count)

    spans = {0: ((10, 18), (10, 18)), 1: ((10, 18), (2, 10)), -1: ((10, 18), (18, 26)),
             2: ((16, 18), (0, 2)), -2: ((10, 12), (26, 28))}

    def raw_copy(w, d, block):
        (s_lo, s_hi), (d_lo, d_hi) = spans[d]
        return remote(
            raw.at[block, s_lo:s_hi],
            raw.at[block, d_lo:d_hi],
            raw_send.at[w, d + 2],
            raw_recv.at[w, d + 2],
            r + d,
            far if w else t,
        )

    def halo_copies(e):
        copies = []
        for d, slot in ((1, 0), (-1, 2)):
            if e == 0:
                src = frames.at[6:8] if d == 1 else frames.at[0:2]
                dst = rp.at[0:2, 16:80] if d == 1 else rp.at[10:12, 16:80]
            else:
                src = hp.at[e - 1, 8, 16:80] if d == 1 else hp.at[e - 1, 1, 16:80]
                dst = hp.at[e - 1, 0, 16:80] if d == 1 else hp.at[e - 1, 9, 16:80]
            copies.append((d, 0, src, dst))
        for dt in (-1, 1):
            own = 0 if dt == -1 else 1
            for d in (0, 1, -1):
                copies.append((d, dt, sbuf.at[e, own], sx.at[e, 1 - own, 1 - d]))
        return [
            (d, dt, remote(src, dst, halo_send.at[e, k], halo_recv.at[e, k], r + d, t + dt))
            for k, (d, dt, src, dst) in enumerate(copies)
        ]

    def start_halo(e):
        for d, dt, copy in halo_copies(e):

            @pl.when(row_ok(d) & col_ok(dt))
            def _():
                copy.start()

    def wait_halo(e):
        for d, dt, copy in halo_copies(e):

            @pl.when(row_ok(-d) & col_ok(-dt))
            def _():
                copy.wait_recv()

    def end_halo(e):
        for d, dt, copy in halo_copies(e):

            @pl.when(row_ok(d) & col_ok(dt))
            def _():
                copy.wait_send()

    def fwd_copy(w, chunk, block):
        lo, hi = ((10, 18), (0, 10), (18, 28))[chunk]
        return remote(
            raw.at[block, lo:hi],
            raw.at[block, lo:hi],
            fwd_send.at[w, chunk],
            fwd_recv.at[w, chunk],
            r,
            sib,
        )

    raw_copy(1, 0, t).start()
    for d in (1, -1):
        for w in (1, 0):

            @pl.when(row_ok(d))
            def _():
                raw_copy(w, d, t).start()

    for d in (2, -2):
        for w in (1, 0):

            @pl.when(row_ok(d))
            def _():
                raw_copy(w, d, t).start()

    fwd_copy(0, 0, t).start()
    start_halo(0)

    for a in range(3):
        for b in range(3):
            wc[a * CH : (a + 1) * CH, b * CH : (b + 1) * CH] = dil_w[3 * a + b]
            wh[a * CH : (a + 1) * CH, 2 * b * CH : 2 * (b + 1) * CH] = gate_w[3 * a + b]
    for k in range(2):
        column = jnp.broadcast_to(mhead_w[:, k : k + 1], (CH, CH))
        for part in range(3):
            rounded = column.astype(BF)
            hw[part * CH : (part + 1) * CH, k * CH : (k + 1) * CH] = rounded
            column = column - rounded.astype(F32)
    embed_one = jnp.concatenate([patch_w[...], jnp.zeros((64, CH), BF)], axis=0)
    embed_two = jnp.concatenate(
        [embed_one, jnp.concatenate([jnp.zeros((64, CH), BF), patch_w[...]], axis=0)], axis=1
    )
    rp[2:10, 16:80] = frames[...]

    def forward(w, chunk, arrivals, block):
        for d in arrivals:
            if w == 0 and d == 0:
                continue

            @pl.when(row_ok(-d))
            def _():
                raw_copy(w, d, block).wait_recv()

        if not (w == 0 and chunk == 0):
            fwd_copy(w, chunk, block).start()

    forward(0, 1, (1, 2), t)
    forward(0, 2, (-1, -2), t)
    forward(1, 0, (0,), far)
    forward(1, 1, (1, 2), far)
    forward(1, 2, (-1, -2), far)

    def embed_block(b):
        pair = dot(raw[b].reshape(28 * 32, CH), embed_two).astype(BF)
        start = pl.multiple_of(b * COLS, 32)
        e1[:, pl.ds(start, 32)] = pair[:, :CH].reshape(28, 32, CH)
        later = pl.multiple_of(b * COLS + 32, 32)
        e1[:, pl.ds(later, 32)] = pair[:, CH:].reshape(28, 32, CH)

    embed_block(t)
    embed_block(far)

    wait_halo(0)
    rp[:, 0:16] = dot(placement(12, 2, 0), sx[0, 0].reshape(48, CH)).astype(BF).reshape(12, 16, CH)
    rp[:, 80:96] = dot(placement(12, 2, 1), sx[0, 1].reshape(48, CH)).astype(BF).reshape(12, 16, CH)
    e0[...] = dot(rp[...].reshape(12 * PADW, CH), embed_one).astype(BF).reshape(12, PADW, CH)
    taps = jnp.concatenate([e0[0:8], e0[2:10], e0[4:12]], axis=2).reshape(BAND * PADW, 3 * CH)
    y = dot(taps, wc[...])
    conv = roll0(y[:, :CH], 2) + y[:, CH : 2 * CH] + roll0(y[:, 2 * CH :], -2)
    conv = conv.reshape(BAND, PADW, CH)[:, 16:80].reshape(BAND * COLS, CH)
    own = e0[2:10, 16:80].reshape(BAND * COLS, CH).astype(F32)
    features = (own + jnp.maximum(conv, 0.0)).astype(BF)
    f0[...] = features
    drive[...] = dot(features, ctx_w[...])

    def share(e, state):
        hp[e - 1, 1:9, 16:80] = state.reshape(BAND, COLS, CH)
        sbuf[e] = dot(pick, state).astype(BF).reshape(2, 16, CH)
        start_halo(e)

    share(1, jnp.tanh(features.astype(F32)).astype(BF))

    for w, chunk in ((0, 0), (0, 1), (0, 2), (1, 0), (1, 1), (1, 2)):
        fwd_copy(w, chunk, far_sib if w else sib).wait_recv()
    embed_block(sib)
    embed_block(far_sib)

    column = lax.broadcasted_iota(jnp.int32, (4 * WIDE, CH), 0) & (WIDE - 1)

    def conv_rows(i, carry):
        y0 = i * 4
        taps = jnp.concatenate(
            [e1[pl.ds(y0, 4)], e1[pl.ds(y0 + 2, 4)], e1[pl.ds(y0 + 4, 4)]], axis=2
        ).reshape(4 * WIDE, 3 * CH)
        y = dot(taps, wc[...])
        before = jnp.where(column < 2, 0.0, roll0(y[:, :CH], 2))
        after = jnp.where(column >= WIDE - 2, 0.0, roll0(y[:, 2 * CH :], -2))
        conv = before + y[:, CH : 2 * CH] + after
        own = e1[pl.ds(y0 + 2, 4)].reshape(4 * WIDE, CH).astype(F32)
        f1[pl.ds(y0, 4)] = (own + jnp.maximum(conv, 0.0)).astype(BF).reshape(4, WIDE, CH)
        return carry

    lax.fori_loop(0, 6, conv_rows, 0)

    scale = LOG2E / math.sqrt(CH)
    rowmax[...] = jnp.full(rowmax.shape, -jnp.inf, F32)
    rowsum[...] = jnp.zeros(rowsum.shape, F32)

    def score_row(j, o):
        s = dot_nt(f0[...], f1[j]) * scale
        sb[j] = s
        rowmax[o] = jnp.maximum(rowmax[o], jnp.maximum(s[:, :CH], s[:, CH:]))
        return o

    for o in range(3):
        lax.fori_loop(8 * o, 8 * o + 8, lambda j, c, o=o: (score_row(j, o), c)[1], 0)

    allowed = []
    for o in range(3):
        ok = (window[0, o] == 1) & row_ok(o - 1)
        allowed.append(ok.astype(jnp.int32))
    tokens = BAND * COLS

    def picked(o, x, other):
        return jnp.where(jnp.full(x.shape, allowed[o]) == 1, x, other)

    top = None
    for o in range(3):
        peak = jnp.max(rowmax[o], axis=1, keepdims=True)
        peak = picked(o, jnp.broadcast_to(peak, (tokens, CH)), -jnp.inf)
        top = peak if top is None else jnp.maximum(top, peak)
    rowmax[0] = top

    def mass_row(j, o):
        peak = rowmax[0]
        s = sb[j]
        rowsum[o] += jnp.exp2(s[:, :CH] - peak) + jnp.exp2(s[:, CH:] - peak)

    for o in range(3):
        lax.fori_loop(8 * o, 8 * o + 8, lambda j, c, o=o: (mass_row(j, o), c)[1], 0)
    total = None
    for o in range(3):
        part = picked(o, rowsum[o], 0.0)
        total = part if total is None else total + part
    total = jnp.broadcast_to(jnp.sum(total, axis=1, keepdims=True), (tokens, CH))
    rowmax[1] = -(rowmax[0] + jnp.log(total) * LOG2E)

    def col_row(j, carry):
        pot = rowmax[1]
        shifted = sb[j] + jnp.concatenate([pot, pot], axis=1)
        peak = jnp.max(shifted, axis=0, keepdims=True)
        q = jnp.exp2(shifted - peak)
        qb[j] = q.astype(BF)
        st[0, pl.ds(j, 1), :] = peak
        st[1, pl.ds(j, 1), :] = jnp.sum(q, axis=0, keepdims=True)
        return carry

    lax.fori_loop(0, 24, col_row, 0)

    col_copies = [
        remote(st, sr.at[k], col_send.at[k], col_recv.at[k], r, peer)
        for k, peer in enumerate((sib, far, far_sib))
    ]
    for copy in col_copies:
        copy.start()
    for copy in col_copies:
        copy.wait_recv()
    peak = jnp.maximum(jnp.maximum(st[0], sr[0, 0]), jnp.maximum(sr[1, 0], sr[2, 0]))
    mine = jnp.exp2(st[0] - peak)
    total = st[1] * mine
    for k in range(3):
        total = total + sr[k, 1] * jnp.exp2(sr[k, 0] - peak)
    factor = mine / total
    for o in range(3):
        gs[8 * o : 8 * o + 8] = picked(o, factor[8 * o : 8 * o + 8], 0.0)

    acc[...] = jnp.zeros(acc.shape, F32)
    sub = lax.broadcasted_iota(jnp.int32, (16, WIDE), 0)
    cell_col = lax.broadcasted_iota(jnp.int32, (16, WIDE), 1).astype(F32)

    def moment_row(j, carry):
        g = jnp.broadcast_to(gs[pl.ds(j, 1), :], (16, WIDE))
        place = jnp.where(sub < 2, 1.0, jnp.where(sub < 4, (j - 8).astype(F32), cell_col))
        weight = jnp.where(sub < 6, g * place, 0.0)
        high = weight.astype(BF).astype(F32)
        weight = jnp.where((sub & 1) == 0, high, weight - high).astype(BF)
        weight = jnp.concatenate([weight, jnp.zeros((CH - 16, WIDE), BF)], axis=0)
        acc[...] += dot_nt(qb[j], weight)
        return carry

    lax.fori_loop(0, 24, moment_row, 0)
    sums = acc[...]

    def column_of(k):
        return jnp.broadcast_to(sums[:, k : k + 1], (tokens, CH))

    token = lax.broadcasted_iota(jnp.int32, (tokens, CH), 0)
    mass = column_of(0) + column_of(1)
    flow_row = (column_of(2) + column_of(3)) / mass - (token >> 6).astype(F32)
    own_col = (token & (COLS - 1)) + t * COLS
    flow_col = (column_of(4) + column_of(5)) / mass - own_col.astype(F32)

    left, right = placement(10, 1, 0), placement(10, 1, 1)
    for it in range(3):
        e = it + 1
        wait_halo(e)
        hp[it, :, 0:16] = dot(left, sx[e, 0].reshape(48, CH)).astype(BF).reshape(10, 16, CH)
        hp[it, :, 80:96] = dot(right, sx[e, 1].reshape(48, CH)).astype(BF).reshape(10, 16, CH)
        taps = jnp.concatenate([hp[it, 0:8], hp[it, 1:9], hp[it, 2:10]], axis=2)
        y = dot(taps.reshape(BAND * PADW, 3 * CH), wh[...])
        gate = roll0(y[:, : 2 * CH], 1) + y[:, 2 * CH : 4 * CH] + roll0(y[:, 4 * CH :], -1)
        gate = gate.reshape(BAND, PADW, 2 * CH)[:, 16:80].reshape(tokens, 2 * CH)

        def pushed(part):
            lanes = slice(part * CH, (part + 1) * CH)
            return (
                drive[:, lanes] + flow_row * mgate_w[0:1, lanes] + flow_col * mgate_w[1:2, lanes]
            )

        update = 0.5 * jnp.tanh(0.5 * (gate[:, :CH] + pushed(0))) + 0.5
        reset = 0.5 * jnp.tanh(0.5 * (gate[:, CH:] + pushed(1))) + 0.5
        hidden = hp[it, 1:9, 16:80].reshape(tokens, CH).astype(F32)
        candidate = jnp.tanh(dot((reset * hidden).astype(BF), cand_w[...]) + pushed(2))
        state = ((1.0 - update) * hidden + update * candidate).astype(BF)
        if it < 2:
            share(e + 1, state)
        step = dot(jnp.concatenate([state, state, state], axis=1), hw[...])
        flow_row = flow_row + step[:, :CH]
        flow_col = flow_col + step[:, CH:]
        if it == 2:
            hidden_out[...] = state.reshape(BAND, COLS, CH)

    lane = lax.broadcasted_iota(jnp.int32, (tokens, CH), 1)
    both = jnp.where(lane == 0, flow_row, flow_col)
    for q in range(4):
        turned = jnp.transpose(both[CH * q : CH * (q + 1)])
        for k in range(2):
            motion_out[k, 2 * q : 2 * q + 1, :] = turned[k : k + 1, 0:COLS]
            motion_out[k, 2 * q + 1 : 2 * q + 2, :] = turned[k : k + 1, COLS:CH]

    for w in range(2):
        for d in (0, 1, -1, 2, -2):
            if w == 0 and d == 0:
                continue

            @pl.when(row_ok(d))
            def _():
                raw_copy(w, d, t).wait_send()

        for chunk in range(3):
            fwd_copy(w, chunk, far if w else t).wait_send()
    for e in range(4):
        end_halo(e)
    for copy in col_copies:
        copy.wait_send()


def on_device(n_rows, *args):
    vmem = pl.BlockSpec(memory_space=pltpu.VMEM)
    smem = pl.BlockSpec(memory_space=pltpu.SMEM)
    tokens = BAND * COLS
    dma = pltpu.SemaphoreType.DMA
    return pl.pallas_call(
        functools.partial(kernel, n_rows),
        out_shape=(
            jax.ShapeDtypeStruct((2, BAND, COLS), F32),
            jax.ShapeDtypeStruct((BAND, COLS, CH), BF),
        ),
        in_specs=[vmem, smem] + [vmem] * 7,
        out_specs=(vmem, vmem),
        scratch_shapes=[
            pltpu.VMEM((4, 28, 32, CH), BF),
            pltpu.VMEM((28, WIDE, CH), BF),
            pltpu.VMEM((24, WIDE, CH), BF),
            pltpu.VMEM((24, tokens, WIDE), F32),
            pltpu.VMEM((24, tokens, WIDE), BF),
            pltpu.VMEM((12, PADW, CH), BF),
            pltpu.VMEM((12, PADW, CH), BF),
            pltpu.VMEM((3, 10, PADW, CH), BF),
            pltpu.VMEM((4, 2, 16, CH), BF),
            pltpu.VMEM((4, 2, 3, 16, CH), BF),
            pltpu.VMEM((2, 24, WIDE), F32),
            pltpu.VMEM((3, 2, 24, WIDE), F32),
            pltpu.VMEM((24, WIDE), F32),
            pltpu.VMEM((3, tokens, CH), F32),
            pltpu.VMEM((3, tokens, CH), F32),
            pltpu.VMEM((tokens, CH), BF),
            pltpu.VMEM((tokens, 3 * CH), F32),
            pltpu.VMEM((3 * CH, 3 * CH), BF),
            pltpu.VMEM((3 * CH, 6 * CH), BF),
            pltpu.VMEM((3 * CH, 2 * CH), BF),
            pltpu.VMEM((tokens, CH), F32),
            dma((2, 5)),
            dma((2, 5)),
            dma((2, 3)),
            dma((2, 3)),
            dma((4, 8)),
            dma((4, 8)),
            dma((3,)),
            dma((3,)),
        ],
        compiler_params=pltpu.CompilerParams(
            collective_id=0, has_side_effects=True, vmem_limit_bytes=52 * 1024 * 1024
        ),
    )(*args)


def solution(mesh):
    in_specs = (P("rows", "tgt", None), P("rows", None), P(), P(), P(), P(), P(), P(), P())
    out_specs = (P(None, "rows", "tgt"), P("rows", "tgt", None))
    return jax.shard_map(
        functools.partial(on_device, mesh.shape["rows"]),
        mesh=mesh,
        in_specs=in_specs,
        out_specs=out_specs,
        check_vma=False,
    )
```

```python
import functools
import math

import jax
import jax.numpy as jnp
from jax import lax
from jax.experimental import pallas as pl
from jax.experimental.pallas import tpu as pltpu
from jax.sharding import PartitionSpec as P

BF = jnp.bfloat16
F32 = jnp.float32
LOG2E = 1.4426950408889634
BAND = 8
COLS = 64
WIDE = 256
CH = 128
PADW = 96
TOKENS = BAND * COLS
LIMIT = 63 * 1024 * 1024
CHUNK = 4 * WIDE


def roll0(x, shift):
    return pltpu.roll(x, shift % x.shape[0], axis=0)


def dot(a, b):
    return jnp.dot(a, b, preferred_element_type=F32)


def dot_nt(a, b):
    return lax.dot_general(a, b, (((1,), (1,)), ((), ())), preferred_element_type=F32)


def one_hot(rows, width, halo, side):
    token = lax.broadcasted_iota(jnp.int32, (rows * width, 48), 0)
    strip = lax.broadcasted_iota(jnp.int32, (rows * width, 48), 1)
    row, col = token // width, token % width
    base = 2 * (row + 8 - halo)
    if width == 16:
        hit = (col >= 14) & (strip == base + col - 14) if side == 0 else (col < 2) & (strip == base + col)
    else:
        hit = (col == 0) & (strip == base + 1) if side == 0 else (col == width - 1) & (strip == base)
    return jnp.where(hit, 1.0, 0.0).astype(BF)


def strip_pick():
    strip = lax.broadcasted_iota(jnp.int32, (32, TOKENS), 0)
    token = lax.broadcasted_iota(jnp.int32, (32, TOKENS), 1)
    row, col = (strip & 15) >> 1, strip & 1
    wanted = row * COLS + col + jnp.where(strip >= 16, COLS - 2, 0)
    return jnp.where(token == wanted, 1.0, 0.0).astype(BF)


def lanes_of(x, times):
    return jnp.concatenate([x] * times, axis=1)


def kernel(
    n_rows,
    frames_in,
    window,
    patch_in,
    dil_in,
    ctx_in,
    gate_in,
    cand_in,
    mgate_in,
    mhead_in,
    motion_out,
    hidden_out,
    frames,
    patch_w,
    dil_w,
    ctx_w,
    gate_w,
    cand_w,
    mgate_w,
    mhead_w,
    pk,
    raw,
    e1,
    f1,
    sb,
    qb,
    rp,
    e0,
    hp,
    sbuf,
    sx,
    st,
    sr,
    cmax,
    rowmax,
    rowsum,
    pot,
    f0,
    drive,
    gpre,
    flow,
    wc,
    hw,
    acc,
    in_sem,
    raw_send,
    raw_recv,
    feat_send,
    feat_recv,
    halo_send,
    halo_recv,
    col_send,
    col_recv,
):
    r = lax.axis_index("rows")
    t = lax.axis_index("tgt")
    core = t % 2
    sib = t + 1 - 2 * core
    far = (t + 2) % 4
    far_sib = 3 - t
    away = 2 * core - 1

    loads = {}
    for k, (src, dst) in enumerate(
        (
            (frames_in, frames),
            (patch_in, patch_w),
            (dil_in, dil_w),
            (ctx_in, ctx_w),
            (gate_in, gate_w),
            (cand_in, cand_w),
            (mgate_in, mgate_w),
            (mhead_in, mhead_w),
        )
    ):
        loads[k] = pltpu.make_async_copy(src, dst, in_sem.at[k])
        loads[k].start()

    def row_ok(d):
        return (r + d >= 0) & (r + d < n_rows)

    def col_ok(d):
        return (t + d >= 0) & (t + d < 4)

    def remote(src, dst, send, recv, rr, tt):
        return pltpu.make_async_remote_copy(
            src_ref=src,
            dst_ref=dst,
            send_sem=send,
            recv_sem=recv,
            device_id=(rr, tt),
            device_id_type=pl.DeviceIdType.MESH,
        )

    barrier = pltpu.get_barrier_semaphore()
    count = 3

    def greet(rr, tt):
        pl.semaphore_signal(
            barrier, inc=1, device_id=(rr, tt), device_id_type=pl.DeviceIdType.MESH
        )

    for d in (1, -1):

        @pl.when(row_ok(d))
        def _():
            for tt in range(4):
                greet(r + d, tt)

        count = count + 4 * row_ok(d).astype(jnp.int32)

    @pl.when(row_ok(2 * away))
    def _():
        for tt in range(4):
            greet(r + 2 * away, tt)

    for d in (2, -2):
        count = count + 2 * row_ok(d).astype(jnp.int32)
    for tt in (far, sib, far_sib):
        greet(r, tt)

    def zero(ref):
        ref[...] = jnp.zeros(ref.shape, ref.dtype)

    near_row, next_row, own_row = 2 + 4 * core, 14 * core, 10 * (1 - core)
    for d, first, n in ((away, near_row, 8), (2 * away, next_row, 2)):

        @pl.when(jnp.logical_not(row_ok(d)))
        def _():
            for b in range(4):
                zero(raw.at[b, pl.ds(first, n)])

    for d, rp_lo, rp_hi, hp_row, slot in ((-1, 0, 2, 0, 0), (1, 10, 12, 9, 2)):

        @pl.when(jnp.logical_not(row_ok(d)))
        def _():
            rp[rp_lo:rp_hi, 16:80] = jnp.zeros((2, COLS, CH), BF)
            for e in range(3):
                hp[e, hp_row] = jnp.zeros((COLS, CH), BF)
            for e in range(4):
                for side in range(2):
                    zero(sx.at[e, side, slot])

    for d, side in ((-1, 0), (1, 1)):

        @pl.when(jnp.logical_not(col_ok(d)))
        def _():
            for e in range(4):
                for slot in range(3):
                    zero(sx.at[e, side, slot])

    loads[0].wait()
    whole = frames[...].astype(F32)
    half0 = whole[:, 0:32].reshape(BAND * 32, CH)
    half1 = whole[:, 32:64].reshape(BAND * 32, CH)
    lane = lax.broadcasted_iota(jnp.int32, (BAND * 32, CH), 1)
    packed = jnp.where(lane < 64, pltpu.roll(half0, 64, axis=1), half1)
    pk[...] = packed.astype(BF).reshape(BAND, 32, CH)
    raw[t, pl.ds(own_row, 6)] = pk[pl.ds(2 * core, 6)]
    pick = strip_pick()
    sbuf[0] = dot(pick, frames[...].reshape(TOKENS, CH)).astype(BF).reshape(2, 16, CH)

    pl.semaphore_wait(barrier, count)

    def raw_copy(src, dst, k, kind, rr, tt):
        return remote(src, dst, raw_send.at[k], raw_recv.at[t, kind], rr, tt)

    raw_sends = []
    k = 0
    for peer, c in ((far, core), (far_sib, 1 - core), (sib, 1 - core)):
        src, dst = pk.at[pl.ds(2 * c, 6)], raw.at[t, pl.ds(10 * (1 - c), 6)]
        raw_sends.append((None, raw_copy(src, dst, k, 0, r, peer)))
        k += 1
    for peer in (0, 2):
        raw_sends.append((1, raw_copy(pk, raw.at[t, 2:10], k, 1, r + 1, peer)))
        raw_sends.append((-1, raw_copy(pk, raw.at[t, 6:14], k + 1, 1, r - 1, peer + 1)))
        k += 2
    for peer in (0, 2):
        raw_sends.append((2, raw_copy(pk.at[6:8], raw.at[t, 0:2], k, 2, r + 2, peer)))
        raw_sends.append((-2, raw_copy(pk.at[0:2], raw.at[t, 14:16], k + 1, 2, r - 2, peer + 1)))
        k += 2

    def when_row(d, act):
        if d is None:
            act()
        else:
            pl.when(row_ok(d))(act)

    for d, copy in raw_sends:
        when_row(d, copy.start)

    def wait_raw(b):
        @pl.when(b != t)
        def _():
            ref = raw.at[b, pl.ds(own_row, 6)]
            remote(ref, ref, raw_send.at[0], raw_recv.at[b, 0], r, sib).wait_recv()

        @pl.when(row_ok(away))
        def _():
            ref = raw.at[b, pl.ds(near_row, 8)]
            remote(ref, ref, raw_send.at[0], raw_recv.at[b, 1], r, sib).wait_recv()

        @pl.when(row_ok(2 * away))
        def _():
            ref = raw.at[b, pl.ds(next_row, 2)]
            remote(ref, ref, raw_send.at[0], raw_recv.at[b, 2], r, sib).wait_recv()

    def halo_copies(e):
        copies = []
        for d in (1, -1):
            if e == 0:
                src = frames.at[6:8] if d == 1 else frames.at[0:2]
                dst = rp.at[0:2, 16:80] if d == 1 else rp.at[10:12, 16:80]
            else:
                src = hp.at[e - 1, 8] if d == 1 else hp.at[e - 1, 1]
                dst = hp.at[e - 1, 0] if d == 1 else hp.at[e - 1, 9]
            copies.append((d, 0, src, dst))
        for dt in (-1, 1):
            own = 0 if dt == -1 else 1
            for d in (1, -1, 0):
                copies.append((d, dt, sbuf.at[e, own], sx.at[e, 1 - own, 1 - d]))
        return [
            (d, dt, remote(src, dst, halo_send.at[e, k], halo_recv.at[e, k], r + d, t + dt))
            for k, (d, dt, src, dst) in enumerate(copies)
        ]

    def start_halo(e):
        for d, dt, copy in halo_copies(e):
            pl.when(row_ok(d) & col_ok(dt))(copy.start)

    def wait_halo(e):
        for d, dt, copy in halo_copies(e):
            pl.when(row_ok(-d) & col_ok(-dt))(copy.wait_recv)

    def end_halo(e):
        for d, dt, copy in halo_copies(e):
            pl.when(row_ok(d) & col_ok(dt))(copy.wait_send)

    start_halo(0)

    for k in range(1, 8):
        loads[k].wait()
    for a in range(3):
        for b in range(3):
            wc[a * CH : (a + 1) * CH, b * CH : (b + 1) * CH] = dil_w[3 * a + b]
    for k in range(2):
        column = jnp.transpose(jnp.broadcast_to(mhead_w[k : k + 1, :], (CH, CH)))
        for part in range(3):
            rounded = column.astype(BF)
            hw[part * CH : (part + 1) * CH, k * CH : (k + 1) * CH] = rounded
            column = column - rounded.astype(F32)
    embed_one = jnp.concatenate([patch_w[...], jnp.zeros((64, CH), BF)], axis=0)
    embed_two = jnp.concatenate(
        [embed_one, jnp.concatenate([jnp.zeros((64, CH), BF), patch_w[...]], axis=0)], axis=1
    )
    rp[2:10, 16:80] = frames[...]

    place0, place1 = one_hot(12, 16, 2, 0), one_hot(12, 16, 2, 1)
    wait_halo(0)
    rp[:, 0:16] = dot(place0, sx[0, 0].reshape(48, CH)).astype(BF).reshape(12, 16, CH)
    rp[:, 80:96] = dot(place1, sx[0, 1].reshape(48, CH)).astype(BF).reshape(12, 16, CH)
    e0[...] = dot(rp[...].reshape(12 * PADW, CH), embed_one).astype(BF).reshape(12, PADW, CH)
    flat = e0[...].reshape(12 * PADW, CH).astype(F32)
    middle = e0[:, 16:80]

    def moved(shift):
        return roll0(flat, shift).reshape(12, PADW, CH)[:, 16:80].astype(BF)

    shifted = (moved(2), middle, moved(-2))
    taps = [shifted[b][2 * a : 2 * a + 8].reshape(TOKENS, CH) for a in range(3) for b in range(3)]
    conv = dot(jnp.concatenate(taps, axis=1), dil_w[...].reshape(9 * CH, CH))
    own = middle[2:10].reshape(TOKENS, CH).astype(F32)
    features = (own + jnp.maximum(conv, 0.0)).astype(BF)
    f0[...] = features
    drive[...] = dot(features, ctx_w[...])

    def share(e, state):
        hp[e - 1, 1:9] = state.reshape(BAND, COLS, CH)
        sbuf[e] = dot(pick, state).astype(BF).reshape(2, 16, CH)
        start_halo(e)

    share(1, jnp.tanh(features.astype(F32)).astype(BF))

    for b in range(4):
        wait_raw(b)
        pair = dot(raw[b].reshape(16 * 32, CH), embed_two).astype(BF)
        e1[:, b * COLS : b * COLS + 32] = pair[:, :CH].reshape(16, 32, CH)
        e1[:, b * COLS + 32 : b * COLS + 64] = pair[:, CH:].reshape(16, 32, CH)

    column = lax.broadcasted_iota(jnp.int32, (CHUNK, CH), 0) & (WIDE - 1)
    feat_copies = [
        remote(f1.at[3 * core + i], f1.at[3 * core + i], feat_send.at[i], feat_recv.at[i], r, sib)
        for i in range(3)
    ]
    for i in range(3):
        rows = [e1[4 * i + 2 * a : 4 * i + 2 * a + 4] for a in range(3)]
        y = dot(jnp.concatenate(rows, axis=2).reshape(CHUNK, 3 * CH), wc[...])
        before = jnp.where(column < 2, 0.0, roll0(y[:, :CH], 2))
        after = jnp.where(column >= WIDE - 2, 0.0, roll0(y[:, 2 * CH :], -2))
        conv = before + y[:, CH : 2 * CH] + after
        own = rows[1].reshape(CHUNK, CH).astype(F32)
        f1[3 * core + i] = (own + jnp.maximum(conv, 0.0)).astype(BF)
        feat_copies[i].start()

    scale = LOG2E / math.sqrt(CH)
    rowmax[...] = jnp.full(rowmax.shape, -jnp.inf, F32)
    rowsum[...] = jnp.zeros(rowsum.shape, F32)

    def score_chunk(c):
        peak = rowmax[c // 2]
        for n in range(4):
            s = dot_nt(f0[...], f1[c, n * WIDE : (n + 1) * WIDE]) * scale
            sb[c, :, n * WIDE : (n + 1) * WIDE] = s
            peak = jnp.maximum(peak, jnp.maximum(s[:, :CH], s[:, CH:]))
        rowmax[c // 2] = peak

    def own_scores(i, carry):
        score_chunk(3 * core + i)
        return carry

    lax.fori_loop(0, 3, own_scores, 0)
    for i in range(3):
        c = 3 * (1 - core) + i
        remote(f1.at[c], f1.at[c], feat_send.at[i], feat_recv.at[i], r, sib).wait_recv()

    def other_scores(i, carry):
        score_chunk(3 * (1 - core) + i)
        return carry

    lax.fori_loop(0, 3, other_scores, 0)

    allowed = []
    for o in range(3):
        ok = (window[0, o] == 1) & row_ok(o - 1)
        allowed.append(ok.astype(jnp.int32))

    def picked(o, x, other):
        return jnp.where(jnp.full(x.shape, allowed[o]) == 1, x, other)

    top = None
    for o in range(3):
        peak = jnp.broadcast_to(jnp.max(rowmax[o], axis=1, keepdims=True), (TOKENS, CH))
        peak = picked(o, peak, -jnp.inf)
        top = peak if top is None else jnp.maximum(top, peak)
    pot[0] = top

    rb = 32

    def eighths(x):
        return x.reshape(rb // 8, 8, CHUNK)

    def mass_chunk(c, carry):
        def block(k, col):
            i = pl.multiple_of(k * rb, rb)
            x = sb[c, pl.ds(i, rb), :] - lanes_of(pot[0, pl.ds(i, rb), :], 8)
            p = jnp.exp2(x)
            parts = [p[:, n * CH : (n + 1) * CH] for n in range(8)]
            while len(parts) > 1:
                parts = [a + b for a, b in zip(parts[::2], parts[1::2])]
            rowsum[c // 2, pl.ds(i, rb), :] += parts[0]
            return jnp.maximum(col, jnp.max(eighths(x), axis=0))

        col = lax.fori_loop(0, TOKENS // rb, block, jnp.full((8, CHUNK), -jnp.inf, F32), unroll=2)
        cmax[c] = jnp.broadcast_to(jnp.max(col, axis=0, keepdims=True), (8, CHUNK))
        return carry

    lax.fori_loop(0, 6, mass_chunk, 0)
    total = None
    for o in range(3):
        part = picked(o, rowsum[o], 0.0)
        total = part if total is None else total + part
    total = jnp.broadcast_to(jnp.sum(total, axis=1, keepdims=True), (TOKENS, CH))
    pot[1] = pot[0] + jnp.log(total) * LOG2E

    def col_chunk(c):
        def block(k, col):
            i = pl.multiple_of(k * rb, rb)
            x = sb[c, pl.ds(i, rb), :] - lanes_of(pot[1, pl.ds(i, rb), :], 8)
            q = jnp.exp2(x - cmax[c, 0:1, :])
            qb[c, pl.ds(i, rb), :] = q.astype(BF)
            return col + jnp.sum(eighths(q), axis=0)

        col = lax.fori_loop(0, TOKENS // rb, block, jnp.zeros((8, CHUNK), F32), unroll=2)
        st[c, 0:1] = cmax[c, 0:1]
        st[c, 1:2] = jnp.sum(col, axis=0, keepdims=True)

    peers = (sib, far, far_sib)

    def col_copy(k, c):
        return remote(st.at[c], sr.at[k, c], col_send.at[k, c], col_recv.at[k, c], r, peers[k])

    def col_step(c, carry):
        col_chunk(c)
        for k in (1, 2, 0):
            col_copy(k, c).start()
        return carry

    lax.fori_loop(0, 6, col_step, 0)

    left, right = one_hot(10, COLS, 1, 0), one_hot(10, COLS, 1, 1)
    edge = lax.broadcasted_iota(jnp.int32, (10 * COLS, CH), 0) & (COLS - 1)

    def gate_conv(e):
        wait_halo(e)
        state = hp[e - 1].reshape(10 * COLS, CH)
        wide = state.astype(F32)
        before = jnp.where(edge == 0, dot(left, sx[e, 0].reshape(48, CH)), roll0(wide, 1))
        after = jnp.where(edge == COLS - 1, dot(right, sx[e, 1].reshape(48, CH)), roll0(wide, -1))
        shifted = (before.astype(BF), state, after.astype(BF))
        taps = [shifted[b][a * COLS : a * COLS + TOKENS] for a in range(3) for b in range(3)]
        conv = dot(jnp.concatenate(taps, axis=1), gate_w[...].reshape(9 * CH, 2 * CH))
        gpre[...] = conv + drive[:, : 2 * CH]

    gate_conv(1)

    sub = lax.broadcasted_iota(jnp.int32, (16, CHUNK), 0)
    cell = lax.broadcasted_iota(jnp.int32, (16, CHUNK), 1)
    cell_row = (cell >> 8).astype(F32)
    cell_col = (cell & (WIDE - 1)).astype(F32)
    acc[...] = jnp.zeros(acc.shape, F32)

    def moment_chunk(c, carry):
        for k in range(3):
            col_copy(k, c).wait_recv()
        peak = jnp.maximum(
            jnp.maximum(st[c, 0:1], sr[0, c, 0:1]), jnp.maximum(sr[1, c, 0:1], sr[2, c, 0:1])
        )
        mine = jnp.exp2(st[c, 0:1] - peak)
        total = st[c, 1:2] * mine
        for k in range(3):
            total = total + sr[k, c, 1:2] * jnp.exp2(sr[k, c, 0:1] - peak)
        factor = mine / total
        open_band = jnp.where(
            c < 2, allowed[0], jnp.where(c < 4, allowed[1], allowed[2])
        )
        factor = jnp.where(jnp.full((1, CHUNK), open_band) == 1, factor, 0.0)
        g = jnp.broadcast_to(factor, (16, CHUNK))
        place = jnp.where(sub < 2, 1.0, jnp.where(sub < 4, cell_row + (4 * c - 8).astype(F32), cell_col))
        weight = jnp.where(sub < 6, g * place, 0.0)
        high = weight.astype(BF).astype(F32)
        weight = jnp.where((sub & 1) == 0, high, weight - high).astype(BF)
        weight = jnp.concatenate([weight, jnp.zeros((CH - 16, CHUNK), BF)], axis=0)
        acc[...] += dot_nt(qb[c], weight)
        return carry

    lax.fori_loop(0, 6, moment_chunk, 0)
    sums = acc[...]

    def column_of(k):
        return jnp.broadcast_to(sums[:, k : k + 1], (TOKENS, CH))

    token = lax.broadcasted_iota(jnp.int32, (TOKENS, CH), 0)
    mass = column_of(0) + column_of(1)
    flow[0] = (column_of(2) + column_of(3)) / mass - (token >> 6).astype(F32)
    own_col = (token & (COLS - 1)) + t * COLS
    flow[1] = (column_of(4) + column_of(5)) / mass - own_col.astype(F32)

    for it in range(3):
        if it > 0:
            gate_conv(it + 1)
        part = 128
        states = []
        for q in range(TOKENS // part):
            at = slice(q * part, (q + 1) * part)
            flow_row, flow_col = flow[0, at], flow[1, at]

            def pushed(n):
                lanes = slice(n * CH, (n + 1) * CH)
                return flow_row * mgate_w[0:1, lanes] + flow_col * mgate_w[1:2, lanes]

            update = 0.5 * jnp.tanh(0.5 * (gpre[at, :CH] + pushed(0))) + 0.5
            reset = 0.5 * jnp.tanh(0.5 * (gpre[at, CH:] + pushed(1))) + 0.5
            hidden = hp[it, 1 + 2 * q : 3 + 2 * q].reshape(part, CH).astype(F32)
            candidate = dot((reset * hidden).astype(BF), cand_w[...])
            candidate = jnp.tanh(candidate + drive[at, 2 * CH :] + pushed(2))
            states.append(((1.0 - update) * hidden + update * candidate).astype(BF))
        state = jnp.concatenate(states, axis=0)
        if it < 2:
            share(it + 2, state)
        else:
            hidden_out[...] = state.reshape(BAND, COLS, CH)
        step = dot(jnp.concatenate([state, state, state], axis=1), hw[...])
        flow[0] += step[:, :CH]
        flow[1] += step[:, CH:]

    lane = lax.broadcasted_iota(jnp.int32, (TOKENS, CH), 1)
    both = jnp.where(lane == 0, flow[0], flow[1])
    for q in range(4):
        turned = jnp.transpose(both[CH * q : CH * (q + 1)])
        for k in range(2):
            motion_out[k, 2 * q : 2 * q + 1, :] = turned[k : k + 1, 0:COLS]
            motion_out[k, 2 * q + 1 : 2 * q + 2, :] = turned[k : k + 1, COLS:CH]

    for d, copy in raw_sends:
        when_row(d, copy.wait_send)
    for copy in feat_copies:
        copy.wait_send()
    for e in range(4):
        end_halo(e)

    def end_col(c, carry):
        for k in range(3):
            col_copy(k, c).wait_send()
        return carry

    lax.fori_loop(0, 6, end_col, 0)


def on_device(n_rows, *args):
    vmem = pl.BlockSpec(memory_space=pltpu.VMEM)
    smem = pl.BlockSpec(memory_space=pltpu.SMEM)
    hbm = pl.BlockSpec(memory_space=pl.ANY)
    dma = pltpu.SemaphoreType.DMA
    args = (*args[:8], args[8].T)
    inputs = [x for k, x in enumerate(args) if k != 1]
    return pl.pallas_call(
        functools.partial(kernel, n_rows),
        out_shape=(
            jax.ShapeDtypeStruct((2, BAND, COLS), F32),
            jax.ShapeDtypeStruct((BAND, COLS, CH), BF),
        ),
        in_specs=[hbm, smem] + [hbm] * 7,
        out_specs=(vmem, vmem),
        scratch_shapes=[pltpu.VMEM(x.shape, x.dtype) for x in inputs]
        + [
            pltpu.VMEM((BAND, 32, CH), BF),
            pltpu.VMEM((4, 16, 32, CH), BF),
            pltpu.VMEM((16, WIDE, CH), BF),
            pltpu.VMEM((6, CHUNK, CH), BF),
            pltpu.VMEM((6, TOKENS, CHUNK), F32),
            pltpu.VMEM((6, TOKENS, CHUNK), BF),
            pltpu.VMEM((12, PADW, CH), BF),
            pltpu.VMEM((12, PADW, CH), BF),
            pltpu.VMEM((3, 10, COLS, CH), BF),
            pltpu.VMEM((4, 2, 16, CH), BF),
            pltpu.VMEM((4, 2, 3, 16, CH), BF),
            pltpu.VMEM((6, 2, CHUNK), F32),
            pltpu.VMEM((3, 6, 2, CHUNK), F32),
            pltpu.VMEM((6, 8, CHUNK), F32),
            pltpu.VMEM((3, TOKENS, CH), F32),
            pltpu.VMEM((3, TOKENS, CH), F32),
            pltpu.VMEM((2, TOKENS, CH), F32),
            pltpu.VMEM((TOKENS, CH), BF),
            pltpu.VMEM((TOKENS, 3 * CH), F32),
            pltpu.VMEM((TOKENS, 2 * CH), F32),
            pltpu.VMEM((2, TOKENS, CH), F32),
            pltpu.VMEM((3 * CH, 3 * CH), BF),
            pltpu.VMEM((3 * CH, 2 * CH), BF),
            pltpu.VMEM((TOKENS, CH), F32),
            dma((8,)),
            dma((11,)),
            dma((4, 3)),
            dma((3,)),
            dma((3,)),
            dma((4, 8)),
            dma((4, 8)),
            dma((3, 6)),
            dma((3, 6)),
        ],
        compiler_params=pltpu.CompilerParams(
            collective_id=0, has_side_effects=True, vmem_limit_bytes=LIMIT
        ),
    )(*args)


def solution(mesh):
    in_specs = (P("rows", "tgt", None), P("rows", None), P(), P(), P(), P(), P(), P(), P())
    out_specs = (P(None, "rows", "tgt"), P("rows", "tgt", None))
    return jax.shard_map(
        functools.partial(on_device, mesh.shape["rows"]),
        mesh=mesh,
        in_specs=in_specs,
        out_specs=out_specs,
        check_vma=False,
    )
```

```python
import functools
import math

import jax
import jax.numpy as jnp
from jax import lax
from jax.experimental import pallas as pl
from jax.experimental.pallas import tpu as pltpu
from jax.sharding import PartitionSpec as P

BF = jnp.bfloat16
F32 = jnp.float32
LOG2E = 1.4426950408889634
BAND = 8
COLS = 64
WIDE = 256
CH = 128
PADW = 96
TOKENS = BAND * COLS
LIMIT = 63 * 1024 * 1024
CHUNK = 4 * WIDE


def roll0(x, shift):
    return pltpu.roll(x, shift % x.shape[0], axis=0)


def dot(a, b):
    return jnp.dot(a, b, preferred_element_type=F32)


def dot_nt(a, b):
    return lax.dot_general(a, b, (((1,), (1,)), ((), ())), preferred_element_type=F32)


def one_hot(rows, halo, side):
    token = lax.broadcasted_iota(jnp.int32, (rows * 16, 48), 0)
    strip = lax.broadcasted_iota(jnp.int32, (rows * 16, 48), 1)
    row, col = token >> 4, token & 15
    base = 2 * (row + 8 - halo)
    if side == 0:
        hit = (col >= 14) & (strip == base + col - 14)
    else:
        hit = (col < 2) & (strip == base + col)
    return jnp.where(hit, 1.0, 0.0).astype(BF)


def strip_pick():
    strip = lax.broadcasted_iota(jnp.int32, (32, TOKENS), 0)
    token = lax.broadcasted_iota(jnp.int32, (32, TOKENS), 1)
    row, col = (strip & 15) >> 1, strip & 1
    wanted = row * COLS + col + jnp.where(strip >= 16, COLS - 2, 0)
    return jnp.where(token == wanted, 1.0, 0.0).astype(BF)


def side_pick(side):
    row = lax.broadcasted_iota(jnp.int32, (48, 48), 0)
    strip = lax.broadcasted_iota(jnp.int32, (48, 48), 1)
    wanted = 2 * ((row & 7) + (row >> 4) + 7) + 1 - side
    return jnp.where((strip == wanted) & ((row & 15) < 8), 1.0, 0.0).astype(BF)


def lanes_of(x, times):
    return jnp.concatenate([x] * times, axis=1)


def kernel(
    n_rows,
    frames_in,
    window,
    patch_in,
    dil_in,
    ctx_in,
    gate_in,
    cand_in,
    mgate_in,
    mhead_in,
    motion_out,
    hidden_out,
    frames,
    patch_w,
    dil_w,
    ctx_w,
    gate_w,
    cand_w,
    mgate_w,
    mhead_w,
    pk,
    raw,
    e1,
    f1,
    sb,
    qb,
    rp,
    e0,
    hp,
    sbuf,
    sx,
    st,
    sr,
    cmax,
    rowmax,
    rowsum,
    pot,
    f0,
    drive,
    gpre,
    flow,
    wc,
    hw,
    acc,
    in_sem,
    raw_send,
    raw_recv,
    feat_send,
    feat_recv,
    halo_send,
    halo_recv,
    col_send,
    col_recv,
):
    r = lax.axis_index("rows")
    t = lax.axis_index("tgt")
    core = t % 2
    sib = t + 1 - 2 * core
    far = (t + 2) % 4
    far_sib = 3 - t
    away = 2 * core - 1

    loads = {}
    for k, (src, dst) in enumerate(
        (
            (frames_in, frames),
            (patch_in, patch_w),
            (dil_in, dil_w),
            (ctx_in, ctx_w),
            (gate_in, gate_w),
            (cand_in, cand_w),
            (mgate_in, mgate_w),
            (mhead_in, mhead_w),
        )
    ):
        loads[k] = pltpu.make_async_copy(src, dst, in_sem.at[k])
        loads[k].start()

    def row_ok(d):
        return (r + d >= 0) & (r + d < n_rows)

    def col_ok(d):
        return (t + d >= 0) & (t + d < 4)

    def remote(src, dst, send, recv, rr, tt):
        return pltpu.make_async_remote_copy(
            src_ref=src,
            dst_ref=dst,
            send_sem=send,
            recv_sem=recv,
            device_id=(rr, tt),
            device_id_type=pl.DeviceIdType.MESH,
        )

    barrier = pltpu.get_barrier_semaphore()
    count = 3

    def greet(rr, tt):
        pl.semaphore_signal(
            barrier, inc=1, device_id=(rr, tt), device_id_type=pl.DeviceIdType.MESH
        )

    for d in (1, -1):

        @pl.when(row_ok(d))
        def _():
            for tt in range(4):
                greet(r + d, tt)

        count = count + 4 * row_ok(d).astype(jnp.int32)

    @pl.when(row_ok(2 * away))
    def _():
        for tt in range(4):
            greet(r + 2 * away, tt)

    for d in (2, -2):
        count = count + 2 * row_ok(d).astype(jnp.int32)
    for tt in (far, sib, far_sib):
        greet(r, tt)

    def zero(ref):
        ref[...] = jnp.zeros(ref.shape, ref.dtype)

    near_row, next_row, own_row = 2 + 4 * core, 14 * core, 10 * (1 - core)
    for d, first, n in ((away, near_row, 8), (2 * away, next_row, 2)):

        @pl.when(jnp.logical_not(row_ok(d)))
        def _():
            for b in range(4):
                zero(raw.at[b, pl.ds(first, n)])

    for d, rp_lo, rp_hi, hp_row, slot in ((-1, 0, 2, 0, 0), (1, 10, 12, 9, 2)):

        @pl.when(jnp.logical_not(row_ok(d)))
        def _():
            rp[rp_lo:rp_hi, 16:80] = jnp.zeros((2, COLS, CH), BF)
            for e in range(3):
                hp[e, hp_row] = jnp.zeros((COLS, CH), BF)
            for e in range(4):
                for side in range(2):
                    zero(sx.at[e, side, slot])

    for d, side in ((-1, 0), (1, 1)):

        @pl.when(jnp.logical_not(col_ok(d)))
        def _():
            for e in range(4):
                for slot in range(3):
                    zero(sx.at[e, side, slot])

    loads[0].wait()
    whole = frames[...].astype(F32)
    half0 = whole[:, 0:32].reshape(BAND * 32, CH)
    half1 = whole[:, 32:64].reshape(BAND * 32, CH)
    lane = lax.broadcasted_iota(jnp.int32, (BAND * 32, CH), 1)
    packed = jnp.where(lane < 64, pltpu.roll(half0, 64, axis=1), half1)
    pk[...] = packed.astype(BF).reshape(BAND, 32, CH)
    raw[t, pl.ds(own_row, 6)] = pk[pl.ds(2 * core, 6)]
    pick = strip_pick()
    sbuf[0] = dot(pick, frames[...].reshape(TOKENS, CH)).astype(BF).reshape(2, 16, CH)

    pl.semaphore_wait(barrier, count)

    def raw_copy(src, dst, k, kind, rr, tt):
        return remote(src, dst, raw_send.at[k], raw_recv.at[t, kind], rr, tt)

    raw_sends = []
    k = 0
    for peer, c in ((far, core), (far_sib, 1 - core), (sib, 1 - core)):
        src, dst = pk.at[pl.ds(2 * c, 6)], raw.at[t, pl.ds(10 * (1 - c), 6)]
        raw_sends.append((None, raw_copy(src, dst, k, 0, r, peer)))
        k += 1
    for peer in (0, 2):
        raw_sends.append((1, raw_copy(pk, raw.at[t, 2:10], k, 1, r + 1, peer)))
        raw_sends.append((-1, raw_copy(pk, raw.at[t, 6:14], k + 1, 1, r - 1, peer + 1)))
        k += 2
    for peer in (0, 2):
        raw_sends.append((2, raw_copy(pk.at[6:8], raw.at[t, 0:2], k, 2, r + 2, peer)))
        raw_sends.append((-2, raw_copy(pk.at[0:2], raw.at[t, 14:16], k + 1, 2, r - 2, peer + 1)))
        k += 2

    def when_row(d, act):
        if d is None:
            act()
        else:
            pl.when(row_ok(d))(act)

    def wait_raw(b):
        @pl.when(b != t)
        def _():
            ref = raw.at[b, pl.ds(own_row, 6)]
            remote(ref, ref, raw_send.at[0], raw_recv.at[b, 0], r, sib).wait_recv()

        @pl.when(row_ok(away))
        def _():
            ref = raw.at[b, pl.ds(near_row, 8)]
            remote(ref, ref, raw_send.at[0], raw_recv.at[b, 1], r, sib).wait_recv()

        @pl.when(row_ok(2 * away))
        def _():
            ref = raw.at[b, pl.ds(next_row, 2)]
            remote(ref, ref, raw_send.at[0], raw_recv.at[b, 2], r, sib).wait_recv()

    def halo_copies(e):
        copies = []
        for d in (1, -1):
            if e == 0:
                src = frames.at[6:8] if d == 1 else frames.at[0:2]
                dst = rp.at[0:2, 16:80] if d == 1 else rp.at[10:12, 16:80]
            else:
                src = hp.at[e - 1, 8] if d == 1 else hp.at[e - 1, 1]
                dst = hp.at[e - 1, 0] if d == 1 else hp.at[e - 1, 9]
            copies.append((d, 0, src, dst))
        for dt in (-1, 1):
            own = 0 if dt == -1 else 1
            for d in (1, -1, 0):
                copies.append((d, dt, sbuf.at[e, own], sx.at[e, 1 - own, 1 - d]))
        return [
            (d, dt, remote(src, dst, halo_send.at[e, k], halo_recv.at[e, k], r + d, t + dt))
            for k, (d, dt, src, dst) in enumerate(copies)
        ]

    def start_halo(e):
        for d, dt, copy in halo_copies(e):
            pl.when(row_ok(d) & col_ok(dt))(copy.start)

    def wait_halo(e):
        for d, dt, copy in halo_copies(e):
            pl.when(row_ok(-d) & col_ok(-dt))(copy.wait_recv)

    def end_halo(e):
        for d, dt, copy in halo_copies(e):
            pl.when(row_ok(d) & col_ok(dt))(copy.wait_send)

    start_halo(0)
    for d, copy in raw_sends:
        when_row(d, copy.start)

    for k in range(1, 8):
        loads[k].wait()
    for a in range(3):
        for b in range(3):
            wc[a * CH : (a + 1) * CH, b * CH : (b + 1) * CH] = dil_w[3 * a + b]
    embed_one = jnp.concatenate([patch_w[...], jnp.zeros((64, CH), BF)], axis=0)
    embed_two = jnp.concatenate(
        [embed_one, jnp.concatenate([jnp.zeros((64, CH), BF), patch_w[...]], axis=0)], axis=1
    )
    rp[2:10, 16:80] = frames[...]
    place0, place1 = one_hot(12, 2, 0), one_hot(12, 2, 1)

    wait_halo(0)
    rp[:, 0:16] = dot(place0, sx[0, 0].reshape(48, CH)).astype(BF).reshape(12, 16, CH)
    rp[:, 80:96] = dot(place1, sx[0, 1].reshape(48, CH)).astype(BF).reshape(12, 16, CH)
    e0[...] = dot(rp[...].reshape(12 * PADW, CH), embed_one).astype(BF).reshape(12, PADW, CH)
    flat = e0[...].reshape(12 * PADW, CH).astype(F32)
    middle = e0[:, 16:80]

    def moved(shift):
        return roll0(flat, shift).reshape(12, PADW, CH)[:, 16:80].astype(BF)

    shifted = (moved(2), middle, moved(-2))
    taps = [shifted[b][2 * a : 2 * a + 8].reshape(TOKENS, CH) for a in range(3) for b in range(3)]
    conv = dot(jnp.concatenate(taps, axis=1), dil_w[...].reshape(9 * CH, CH))
    own = middle[2:10].reshape(TOKENS, CH).astype(F32)
    features = (own + jnp.maximum(conv, 0.0)).astype(BF)
    f0[...] = features
    drive[...] = dot(features, ctx_w[...])

    def share(e, state):
        hp[e - 1, 1:9] = state.reshape(BAND, COLS, CH)
        sbuf[e] = dot(pick, state).astype(BF).reshape(2, 16, CH)
        start_halo(e)

    share(1, jnp.tanh(features.astype(F32)).astype(BF))

    for k in range(2):
        column = jnp.transpose(jnp.broadcast_to(mhead_w[k : k + 1, :], (CH, CH)))
        for part in range(3):
            rounded = column.astype(BF)
            hw[part * CH : (part + 1) * CH, k * CH : (k + 1) * CH] = rounded
            column = column - rounded.astype(F32)

    for b in range(4):
        wait_raw(b)
        pair = dot(raw[b].reshape(16 * 32, CH), embed_two).astype(BF)
        e1[:, b * COLS : b * COLS + 32] = pair[:, :CH].reshape(16, 32, CH)
        e1[:, b * COLS + 32 : b * COLS + 64] = pair[:, CH:].reshape(16, 32, CH)

    column = lax.broadcasted_iota(jnp.int32, (CHUNK, CH), 0) & (WIDE - 1)
    feat_copies = [
        remote(f1.at[3 * core + i], f1.at[3 * core + i], feat_send.at[i], feat_recv.at[i], r, sib)
        for i in range(3)
    ]
    for i in range(3):
        rows = [e1[4 * i + 2 * a : 4 * i + 2 * a + 4] for a in range(3)]
        y = dot(jnp.concatenate(rows, axis=2).reshape(CHUNK, 3 * CH), wc[...])
        before = jnp.where(column < 2, 0.0, roll0(y[:, :CH], 2))
        after = jnp.where(column >= WIDE - 2, 0.0, roll0(y[:, 2 * CH :], -2))
        conv = before + y[:, CH : 2 * CH] + after
        own = rows[1].reshape(CHUNK, CH).astype(F32)
        f1[3 * core + i] = (own + jnp.maximum(conv, 0.0)).astype(BF)
        feat_copies[i].start()

    scale = LOG2E / math.sqrt(CH)
    rowmax[...] = jnp.full(rowmax.shape, -jnp.inf, F32)
    rowsum[...] = jnp.zeros(rowsum.shape, F32)

    def score_chunk(c):
        peak = rowmax[c // 2]
        for n in range(4):
            s = dot_nt(f0[...], f1[c, n * WIDE : (n + 1) * WIDE]) * scale
            sb[c, :, n * WIDE : (n + 1) * WIDE] = s
            peak = jnp.maximum(peak, jnp.maximum(s[:, :CH], s[:, CH:]))
        rowmax[c // 2] = peak

    def own_scores(i, carry):
        score_chunk(3 * core + i)
        return carry

    lax.fori_loop(0, 3, own_scores, 0)
    for i in range(3):
        c = 3 * (1 - core) + i
        remote(f1.at[c], f1.at[c], feat_send.at[i], feat_recv.at[i], r, sib).wait_recv()

    def other_scores(i, carry):
        score_chunk(3 * (1 - core) + i)
        return carry

    lax.fori_loop(0, 3, other_scores, 0)

    allowed = []
    for o in range(3):
        ok = (window[0, o] == 1) & row_ok(o - 1)
        allowed.append(ok.astype(jnp.int32))

    def picked(o, x, other):
        return jnp.where(jnp.full(x.shape, allowed[o]) == 1, x, other)

    top = None
    for o in range(3):
        peak = jnp.broadcast_to(jnp.max(rowmax[o], axis=1, keepdims=True), (TOKENS, CH))
        peak = picked(o, peak, -jnp.inf)
        top = peak if top is None else jnp.maximum(top, peak)
    pot[0] = top

    rb = 32

    def eighths(x):
        return x.reshape(rb // 8, 8, CHUNK)

    def mass_chunk(c, carry):
        def block(k, col):
            i = pl.multiple_of(k * rb, rb)
            x = sb[c, pl.ds(i, rb), :] - lanes_of(pot[0, pl.ds(i, rb), :], 8)
            p = jnp.exp2(x)
            parts = [p[:, n * CH : (n + 1) * CH] for n in range(8)]
            while len(parts) > 1:
                parts = [a + b for a, b in zip(parts[::2], parts[1::2])]
            rowsum[c // 2, pl.ds(i, rb), :] += parts[0]
            return jnp.maximum(col, jnp.max(eighths(x), axis=0))

        col = lax.fori_loop(0, TOKENS // rb, block, jnp.full((8, CHUNK), -jnp.inf, F32), unroll=4)
        cmax[c] = jnp.broadcast_to(jnp.max(col, axis=0, keepdims=True), (8, CHUNK))
        return carry

    lax.fori_loop(0, 6, mass_chunk, 0)
    total = None
    for o in range(3):
        part = picked(o, rowsum[o], 0.0)
        total = part if total is None else total + part
    total = jnp.broadcast_to(jnp.sum(total, axis=1, keepdims=True), (TOKENS, CH))
    pot[1] = pot[0] + jnp.log(total) * LOG2E

    def col_chunk(c):
        def block(k, col):
            i = pl.multiple_of(k * rb, rb)
            x = sb[c, pl.ds(i, rb), :] - lanes_of(pot[1, pl.ds(i, rb), :], 8)
            q = jnp.exp2(x - cmax[c, 0:1, :])
            qb[c, pl.ds(i, rb), :] = q.astype(BF)
            return col + jnp.sum(eighths(q), axis=0)

        col = lax.fori_loop(0, TOKENS // rb, block, jnp.zeros((8, CHUNK), F32), unroll=4)
        st[c, 0:1] = cmax[c, 0:1]
        st[c, 1:2] = jnp.sum(col, axis=0, keepdims=True)

    peers = (sib, far, far_sib)

    def col_copy(k, c):
        return remote(st.at[c], sr.at[k, c], col_send.at[k, c], col_recv.at[k, c], r, peers[k])

    def col_step(c, carry):
        col_chunk(c)
        for k in (1, 2, 0):
            col_copy(k, c).start()
        return carry

    lax.fori_loop(0, 6, col_step, 0)

    edge = lax.broadcasted_iota(jnp.int32, (TOKENS, CH), 0) & (COLS - 1)
    picks = (side_pick(0), side_pick(1))
    border = jnp.zeros((COLS, CH), BF)

    def beside(x, n):
        wide, at = x.astype(F32), edge[:n]
        before = jnp.where(at == 0, 0.0, roll0(wide, 1)).astype(BF)
        after = jnp.where(at == COLS - 1, 0.0, roll0(wide, -1)).astype(BF)
        return before, x, after

    def own_gates(state):
        taps = []
        shifted = beside(state, TOKENS)
        for a in range(3):
            for x in shifted:
                if a == 0:
                    x = jnp.concatenate([border, x[: TOKENS - COLS]], axis=0)
                elif a == 2:
                    x = jnp.concatenate([x[COLS:], border], axis=0)
                taps.append(x)
        conv = dot(jnp.concatenate(taps, axis=1), gate_w[...].reshape(9 * CH, 2 * CH))
        gpre[...] = conv + drive[:, : 2 * CH]

    def edge_gates(e):
        wait_halo(e)
        for a, row, at in ((0, 0, 0), (2, 9, TOKENS - COLS)):
            x = jnp.concatenate(beside(hp[e - 1, row], COLS), axis=1)
            w = gate_w[3 * a : 3 * a + 3].reshape(3 * CH, 2 * CH)
            gpre[at : at + COLS] += dot(x, w)
        for side, b, at in ((0, 0, 0), (1, 2, COLS - 1)):
            x = dot(picks[side], sx[e, side].reshape(48, CH)).astype(BF)
            x = jnp.concatenate([x[0:8], x[16:24], x[32:40]], axis=1)
            w = jnp.concatenate([gate_w[b], gate_w[3 + b], gate_w[6 + b]], axis=0)
            extra = dot(x, w)
            for y in range(BAND):
                i = y * COLS + at
                gpre[i : i + 1] += extra[y : y + 1]

    own_gates(hp[0, 1:9].reshape(TOKENS, CH))
    edge_gates(1)

    sub = lax.broadcasted_iota(jnp.int32, (16, CHUNK), 0)
    cell = lax.broadcasted_iota(jnp.int32, (16, CHUNK), 1)
    cell_row = (cell >> 8).astype(F32)
    cell_col = (cell & (WIDE - 1)).astype(F32)
    acc[...] = jnp.zeros(acc.shape, F32)

    def moment_chunk(c, carry):
        for k in range(3):
            col_copy(k, c).wait_recv()
        peak = jnp.maximum(
            jnp.maximum(st[c, 0:1], sr[0, c, 0:1]), jnp.maximum(sr[1, c, 0:1], sr[2, c, 0:1])
        )
        mine = jnp.exp2(st[c, 0:1] - peak)
        total = st[c, 1:2] * mine
        for k in range(3):
            total = total + sr[k, c, 1:2] * jnp.exp2(sr[k, c, 0:1] - peak)
        factor = mine / total
        open_band = jnp.where(
            c < 2, allowed[0], jnp.where(c < 4, allowed[1], allowed[2])
        )
        factor = jnp.where(jnp.full((1, CHUNK), open_band) == 1, factor, 0.0)
        g = jnp.broadcast_to(factor, (16, CHUNK))
        place = jnp.where(sub < 2, 1.0, jnp.where(sub < 4, cell_row + (4 * c - 8).astype(F32), cell_col))
        weight = jnp.where(sub < 6, g * place, 0.0)
        high = weight.astype(BF).astype(F32)
        weight = jnp.where((sub & 1) == 0, high, weight - high).astype(BF)
        weight = jnp.concatenate([weight, jnp.zeros((CH - 16, CHUNK), BF)], axis=0)
        acc[...] += dot_nt(qb[c], weight)
        return carry

    lax.fori_loop(0, 6, moment_chunk, 0)
    sums = acc[...]

    def column_of(k):
        return jnp.broadcast_to(sums[:, k : k + 1], (TOKENS, CH))

    token = lax.broadcasted_iota(jnp.int32, (TOKENS, CH), 0)
    mass = column_of(0) + column_of(1)
    flow[0] = (column_of(2) + column_of(3)) / mass - (token >> 6).astype(F32)
    own_col = (token & (COLS - 1)) + t * COLS
    flow[1] = (column_of(4) + column_of(5)) / mass - own_col.astype(F32)

    for it in range(3):
        if it > 0:
            edge_gates(it + 1)
        part = 128
        states = []
        for q in range(TOKENS // part):
            at = slice(q * part, (q + 1) * part)
            flow_row, flow_col = flow[0, at], flow[1, at]

            def pushed(n):
                lanes = slice(n * CH, (n + 1) * CH)
                return flow_row * mgate_w[0:1, lanes] + flow_col * mgate_w[1:2, lanes]

            update = 0.5 * jnp.tanh(0.5 * (gpre[at, :CH] + pushed(0))) + 0.5
            reset = 0.5 * jnp.tanh(0.5 * (gpre[at, CH:] + pushed(1))) + 0.5
            hidden = hp[it, 1 + 2 * q : 3 + 2 * q].reshape(part, CH).astype(F32)
            candidate = dot((reset * hidden).astype(BF), cand_w[...])
            candidate = jnp.tanh(candidate + drive[at, 2 * CH :] + pushed(2))
            states.append(((1.0 - update) * hidden + update * candidate).astype(BF))
        state = jnp.concatenate(states, axis=0)
        if it < 2:
            share(it + 2, state)
        else:
            hidden_out[...] = state.reshape(BAND, COLS, CH)
        step = dot(jnp.concatenate([state, state, state], axis=1), hw[...])
        flow[0] += step[:, :CH]
        flow[1] += step[:, CH:]
        if it < 2:
            own_gates(state)

    lane = lax.broadcasted_iota(jnp.int32, (TOKENS, CH), 1)
    both = jnp.where(lane == 0, flow[0], flow[1])
    for q in range(4):
        turned = jnp.transpose(both[CH * q : CH * (q + 1)])
        for k in range(2):
            motion_out[k, 2 * q : 2 * q + 1, :] = turned[k : k + 1, 0:COLS]
            motion_out[k, 2 * q + 1 : 2 * q + 2, :] = turned[k : k + 1, COLS:CH]

    for d, copy in raw_sends:
        when_row(d, copy.wait_send)
    for copy in feat_copies:
        copy.wait_send()
    for e in range(4):
        end_halo(e)

    def end_col(c, carry):
        for k in range(3):
            col_copy(k, c).wait_send()
        return carry

    lax.fori_loop(0, 6, end_col, 0)


def on_device(n_rows, *args):
    vmem = pl.BlockSpec(memory_space=pltpu.VMEM)
    smem = pl.BlockSpec(memory_space=pltpu.SMEM)
    hbm = pl.BlockSpec(memory_space=pl.ANY)
    dma = pltpu.SemaphoreType.DMA
    args = (*args[:8], args[8].T)
    inputs = [x for k, x in enumerate(args) if k != 1]
    return pl.pallas_call(
        functools.partial(kernel, n_rows),
        out_shape=(
            jax.ShapeDtypeStruct((2, BAND, COLS), F32),
            jax.ShapeDtypeStruct((BAND, COLS, CH), BF),
        ),
        in_specs=[hbm, smem] + [hbm] * 7,
        out_specs=(vmem, vmem),
        scratch_shapes=[pltpu.VMEM(x.shape, x.dtype) for x in inputs]
        + [
            pltpu.VMEM((BAND, 32, CH), BF),
            pltpu.VMEM((4, 16, 32, CH), BF),
            pltpu.VMEM((16, WIDE, CH), BF),
            pltpu.VMEM((6, CHUNK, CH), BF),
            pltpu.VMEM((6, TOKENS, CHUNK), F32),
            pltpu.VMEM((6, TOKENS, CHUNK), BF),
            pltpu.VMEM((12, PADW, CH), BF),
            pltpu.VMEM((12, PADW, CH), BF),
            pltpu.VMEM((3, 10, COLS, CH), BF),
            pltpu.VMEM((4, 2, 16, CH), BF),
            pltpu.VMEM((4, 2, 3, 16, CH), BF),
            pltpu.VMEM((6, 2, CHUNK), F32),
            pltpu.VMEM((3, 6, 2, CHUNK), F32),
            pltpu.VMEM((6, 8, CHUNK), F32),
            pltpu.VMEM((3, TOKENS, CH), F32),
            pltpu.VMEM((3, TOKENS, CH), F32),
            pltpu.VMEM((2, TOKENS, CH), F32),
            pltpu.VMEM((TOKENS, CH), BF),
            pltpu.VMEM((TOKENS, 3 * CH), F32),
            pltpu.VMEM((TOKENS, 2 * CH), F32),
            pltpu.VMEM((2, TOKENS, CH), F32),
            pltpu.VMEM((3 * CH, 3 * CH), BF),
            pltpu.VMEM((3 * CH, 2 * CH), BF),
            pltpu.VMEM((TOKENS, CH), F32),
            dma((8,)),
            dma((11,)),
            dma((4, 3)),
            dma((3,)),
            dma((3,)),
            dma((4, 8)),
            dma((4, 8)),
            dma((3, 6)),
            dma((3, 6)),
        ],
        compiler_params=pltpu.CompilerParams(
            collective_id=0, has_side_effects=True, vmem_limit_bytes=LIMIT
        ),
    )(*args)


def solution(mesh):
    in_specs = (P("rows", "tgt", None), P("rows", None), P(), P(), P(), P(), P(), P(), P())
    out_specs = (P(None, "rows", "tgt"), P("rows", "tgt", None))
    return jax.shard_map(
        functools.partial(on_device, mesh.shape["rows"]),
        mesh=mesh,
        in_specs=in_specs,
        out_specs=out_specs,
        check_vma=False,
    )
```
